512 devices in a mesh: tm: 64 (over z, y), state: 8 (over x, core).
Axes of the slice: x: 4, y: 8, z: 8, core: 2. Of those that a mesh axis runs over, the one named last changes fastest.
Arguments:
- offsets: int32 [5], replicated, may hold values from -3 to 3
- coefficients: float32 [5, 2048], replicated, may hold values from 0.1 to 1
- gain_matrix: bfloat16 [64, 1, 2048, 512], P('tm', None, 'state'), may hold values from -0.0625 to 0.0625
- direct_gain: float32 [64, 1, 512], P('tm'), may hold values from 0.2 to 0.8
- observed_cells: int32 [64, 1, 512], P('tm'), may hold values from 0 to 2047
- observed_values: float32 [64, 1, 512], P('tm'), may hold values from -4 to 4
Outputs:
- transition: float32 [64, 2048, 2048], P('tm', None, 'state')
- offset_term: float32 [64, 2048], P('tm')
The draws below stay inside these ranges and needn't reach their ends.
All inputs are finite; a program needn't handle non-finite values.
Results may differ from the reference program's by a relative error of at most 0.0036.
Values may be sent and summed in bfloat16 or wider, within the bound.
A program may use at most 64 MiB of HBM per device.

```python
import math
import jax
import jax.numpy as jnp
from jax import lax

D = 2048
OBS = 512
STEPS = 1
NB = 5
NCH = 64


def place_ends(result, key, least, largest):
    longest = result.shape.index(max(result.shape))
    spots = []
    for shift in (0, 1):
        where = [jax.random.randint(jax.random.fold_in(key, axis), (), 0, length) for axis, length in enumerate(result.shape)]
        where[longest] = (where[longest] + shift) % result.shape[longest]
        spots.append(tuple(where))
    return result.at[spots[0]].set(least).at[spots[1]].set(largest)


def steps_of(own_key, shape, split, smallest, top_value):
    loudness, own = 1.0, jax.random.fold_in(own_key, 6)
    for position, shards_of in split:
        heights = jnp.exp(jax.random.uniform(jax.random.fold_in(own, position), (shards_of,), jnp.float32, smallest / len(split), top_value / len(split)))
        loudness = loudness * jnp.repeat(heights, shape[position] // shards_of).reshape([-1 if axis == position else 1 for axis in range(len(shape))])
    return loudness


def centred(own_key, dims, scale, most, cuts=(), held_as=jnp.bfloat16):
    array = scale * jax.random.normal(own_key, dims, jnp.float32)
    if cuts:
        array = array * steps_of(own_key, dims, cuts, -0.22, 0.18)
    return jnp.clip(array, -most, most).astype(held_as)


def setup_inputs(seed: int = 0) -> dict:
    arg_keys = jax.random.split(jax.random.key(seed), 7)
    return {
        "offsets": place_ends(jax.random.randint(arg_keys[0], (NB,), -3, 4), jax.random.fold_in(arg_keys[0], 1), -3, 3).astype(jnp.int32),
        "coefficients": jnp.clip(jnp.exp(jax.random.uniform(arg_keys[1], (NB, D), jnp.float32, math.log(0.1), math.log(1.0))), 0.1, 1.0),
        "gain_matrix": centred(arg_keys[2], (NCH, STEPS, D, OBS), (4 * D) ** -0.5, 0.0625, ((0, 64), (2, 8))),
        "direct_gain": jnp.clip(0.2 + 0.6 * jax.random.uniform(arg_keys[3], (NCH, STEPS, OBS), jnp.float32) ** steps_of(arg_keys[3], (NCH, STEPS, OBS), ((0, 64),), -0.2, 0.2), 0.2, 0.8),
        "observed_cells": place_ends(jax.random.randint(arg_keys[4], (NCH, STEPS, OBS), 0, D), jax.random.fold_in(arg_keys[4], 1), 0, D - 1).astype(jnp.int32),
        "observed_values": centred(arg_keys[5], (NCH, STEPS, OBS), 1.0, 4.0, ((0, 64),), jnp.float32),
    }


def build_table(gain_block, direct_block, cell_block):
    cell_ids = lax.broadcasted_iota(jnp.int32, gain_block.shape, 1)
    observed_hit = cell_ids == cell_block[:, None, :]
    extra = jnp.where(observed_hit, direct_block[:, None, :], jnp.zeros_like(direct_block[:, None, :]))
    return (gain_block.astype(jnp.float32) + extra).astype(jnp.bfloat16)


def advance(matrix, step_gains, cells_used, weights, offsets, forcing):
    for step_index in range(step_gains.shape[0]):
        spread = weights[0][:, None] * jnp.roll(matrix, -offsets[0], axis=0)
        for tap_index in range(1, weights.shape[0]):
            spread = spread + weights[tap_index][:, None] * jnp.roll(matrix, -offsets[tap_index], axis=0)
        picked = jnp.take(spread, cells_used[step_index], axis=0)
        if forcing is not None:
            picked = picked - forcing[step_index][:, None]
        correction = jnp.dot(step_gains[step_index], picked.astype(jnp.bfloat16), preferred_element_type=jnp.float32)
        matrix = spread - correction
    return matrix


def reference(offsets, coefficients, gain_matrix, direct_gain, observed_cells, observed_values):
    weights = coefficients / jnp.sum(coefficients, axis=0, keepdims=True)

    def span_map(span_id, matrix, forced):
        clamped = jnp.maximum(span_id, 0).astype(jnp.int32)
        step_gains = build_table(gain_matrix[clamped], direct_gain[clamped], observed_cells[clamped])
        forcing = observed_values[clamped] if forced else None
        return advance(matrix, step_gains, observed_cells[clamped], weights, offsets, forcing)

    spans = jnp.arange(NCH, dtype=jnp.int32)
    zero_column = jnp.zeros((D, 1), jnp.float32)
    level_zero = lax.map(lambda span_id: span_map(span_id, zero_column, True), spans)

    def level_one_fn(span_id):
        earlier = level_zero[jnp.maximum(span_id - 1, 0)]
        carried = span_map(span_id, earlier, False) + level_zero[span_id]
        return jnp.where(span_id >= 1, carried, level_zero[span_id])

    level_one = lax.map(level_one_fn, spans)

    def level_two_fn(span_id):
        earlier = level_one[jnp.maximum(span_id - 2, 0)]
        carried = span_map(span_id, span_map(span_id - 1, earlier, False), False) + level_one[span_id]
        return jnp.where(span_id >= 2, carried, level_one[span_id])

    offset_term = lax.map(level_two_fn, spans)[:, :, 0]
    identity = jnp.eye(D, dtype=jnp.float32)

    def transition_fn(span_id):
        current = identity
        for distance in (3, 2, 1, 0):
            source = span_id - distance
            current = lax.cond(source >= 0, lambda held: span_map(source, held, False), lambda held: held, current)
        return current

    transition = lax.map(transition_fn, spans)
    return transition, offset_term
```

```python
import functools

import jax
import jax.numpy as jnp
from jax import lax
from jax.experimental import pallas as pl
from jax.experimental.pallas import tpu as pltpu
from jax.sharding import PartitionSpec as P

REACH = 3
TAPS = 2 * REACH + 1
PAD = 8
LEVELS = 4
LANES = 128
CHUNK = 64
VMEM_SPEC = pl.BlockSpec(memory_space=pltpu.VMEM)


def from_behind(value, axis, steps):
    count = lax.axis_size(axis)
    return lax.ppermute(value, axis, [(source, source + steps) for source in range(count - steps)])


def dense_taps(offsets, coefficients):
    weights = coefficients / jnp.sum(coefficients, axis=0, keepdims=True)
    places = jnp.arange(-REACH, REACH + 1, dtype=offsets.dtype)
    hits = places[:, None] == offsets[None, :]
    taps = jnp.sum(jnp.where(hits[:, :, None], weights[None], 0.0), axis=1)
    return jnp.pad(taps, ((0, 8 - TAPS), (0, 0))).T


def local_gain_rows(gain_matrix, direct_gain, observed_cells):
    row_count = gain_matrix.shape[2]
    first_row = lax.axis_index("state") * row_count
    cell_ids = first_row + lax.broadcasted_iota(jnp.int32, gain_matrix.shape[2:], 0)
    observed_hit = cell_ids == observed_cells[0]
    extra = jnp.where(observed_hit, direct_gain[0], 0.0)
    return (gain_matrix[0, 0].astype(jnp.float32) + extra).astype(jnp.bfloat16)


def spread_weights(taps_ref, wide_ref):
    @pl.loop(0, wide_ref.shape[1] // CHUNK)
    def _(i):
        rows = pl.ds(pl.multiple_of(i * CHUNK, CHUNK), CHUNK)
        block = taps_ref[rows, :]
        for j in range(TAPS):
            wide_ref[j, rows, :] = jnp.broadcast_to(block[:, j : j + 1], (CHUNK, LANES))


def start_panel(x_ref, first_column):
    groups, padded, _ = x_ref.shape
    cells = padded - 2 * PAD

    @pl.loop(0, padded // PAD)
    def _(i):
        row = i * PAD - PAD + lax.broadcasted_iota(jnp.int32, (PAD, LANES), 0)
        row = jnp.where(row < 0, row + cells, jnp.where(row >= cells, row - cells, row))
        column = first_column + lax.broadcasted_iota(jnp.int32, (PAD, LANES), 1)
        rows = pl.ds(pl.multiple_of(i * PAD, PAD), PAD)
        for g in range(groups - 1):
            x_ref[g, rows, :] = (row == column + g * LANES).astype(jnp.float32)
        x_ref[groups - 1, rows, :] = jnp.zeros((PAD, LANES), jnp.float32)


def span_step(gains, cells_ref, values_ref, wide_ref, x_ref, y_ref, low_ref, hot_ref, picked_ref, store):
    groups, padded, _ = x_ref.shape
    cells = padded - 2 * PAD
    obs = picked_ref.shape[0]

    @pl.loop(0, cells // CHUNK)
    def _(i):
        base = pl.multiple_of(i * CHUNK, CHUNK)
        rows = pl.ds(base, CHUNK)
        for g in range(groups):
            total = None
            for j in range(TAPS):
                part = wide_ref[j, rows, :] * x_ref[g, pl.ds(base + (PAD - REACH + j), CHUNK), :]
                total = part if total is None else total + part
            y_ref[g, rows, :] = total
            low_ref[rows, g * LANES : (g + 1) * LANES] = total.astype(jnp.bfloat16)

    wanted = cells_ref[...]

    for b in range(cells // obs):
        ids = b * obs + lax.broadcasted_iota(jnp.int32, (obs, obs), 1)
        hot_ref[:, b * obs : (b + 1) * obs] = (ids == wanted).astype(jnp.bfloat16)
    picked_ref[:, : groups * LANES] = jnp.dot(
        hot_ref[...], low_ref[...], preferred_element_type=jnp.float32
    ).astype(jnp.bfloat16)
    lane = lax.broadcasted_iota(jnp.int32, (obs, LANES), 1)
    picked_ref[:, groups * LANES :] = jnp.where(lane == 0, -values_ref[...], 0.0).astype(jnp.bfloat16)

    block = 256

    @pl.loop(0, cells // block)
    def _(i):
        base = pl.multiple_of(i * block, block)
        rows = pl.ds(base, block)
        correction = jnp.dot(gains(base, block), picked_ref[...], preferred_element_type=jnp.float32)
        for g in range(groups):
            value = y_ref[g, rows, :] - correction[:, g * LANES : (g + 1) * LANES]
            if g == groups - 1:
                value = value - correction[:, groups * LANES :]
            store(g, base, block, value)


def compute_kernel(taps_ref, gains_ref, cells_ref, values_ref, out_ref, offset_ref,
                   wide_ref, x_ref, y_ref, low_ref, hot_ref, picked_ref):
    span = lax.axis_index("tm")
    cells = out_ref.shape[0]
    groups = x_ref.shape[0]
    first_column = lax.axis_index("state") * out_ref.shape[1]
    spread_weights(taps_ref, wide_ref)
    start_panel(x_ref, first_column)

    def keep(g, base, block, value):
        x_ref[g, pl.ds(base + PAD, block), :] = value

    def finish(g, base, block, value):
        if g < groups - 1:
            out_ref[pl.ds(base, block), g * LANES : (g + 1) * LANES] = value
        else:
            for part in range(block // LANES):
                square = value[part * LANES : (part + 1) * LANES, :].T
                offset_ref[0:1, pl.ds(pl.multiple_of(base + part * LANES, LANES), LANES)] = square[0:1, :]

    for behind in range(LEVELS - 1, -1, -1):
        def run(behind=behind):
            span_step(
                lambda base, block: gains_ref[behind, pl.ds(base, block), :],
                cells_ref.at[behind], values_ref.at[behind],
                wide_ref, x_ref, y_ref, low_ref, hot_ref, picked_ref,
                keep if behind else finish,
            )
            if behind:
                for g in range(groups):
                    x_ref[g, 0:PAD, :] = x_ref[g, cells : cells + PAD, :]
                    x_ref[g, cells + PAD : cells + 2 * PAD, :] = x_ref[g, PAD : 2 * PAD, :]

        if behind:
            pl.when(span >= behind)(run)
        else:
            run()


def shards(offsets, coefficients, gain_matrix, direct_gain, observed_cells, observed_values):
    taps = dense_taps(offsets, coefficients)
    rows = local_gain_rows(gain_matrix, direct_gain, observed_cells)
    near = lambda value: jnp.stack([value] + [from_behind(value, "tm", k) for k in range(1, LEVELS)])
    gains = lax.all_gather(near(rows), "state", axis=1, tiled=True)
    cells_used = near(observed_cells[0, 0][:, None])
    values = near(observed_values[0, 0][:, None])
    cells, obs = gains.shape[1:]
    columns = rows.shape[0]
    groups = columns // LANES + 1
    out, offset = pl.pallas_call(
        compute_kernel,
        out_shape=(
            jax.ShapeDtypeStruct((cells, columns), jnp.float32),
            jax.ShapeDtypeStruct((1, cells), jnp.float32),
        ),
        in_specs=[VMEM_SPEC] * 4,
        out_specs=(VMEM_SPEC, VMEM_SPEC),
        scratch_shapes=[
            pltpu.VMEM((TAPS, cells, LANES), jnp.float32),
            pltpu.VMEM((groups, cells + 2 * PAD, LANES), jnp.float32),
            pltpu.VMEM((groups, cells, LANES), jnp.float32),
            pltpu.VMEM((cells, groups * LANES), jnp.bfloat16),
            pltpu.VMEM((obs, cells), jnp.bfloat16),
            pltpu.VMEM((obs, (groups + 1) * LANES), jnp.bfloat16),
        ],
        compiler_params=pltpu.CompilerParams(vmem_limit_bytes=56 * 1024 * 1024),
    )(taps, gains, cells_used, values)
    return out[None], offset


def solution(mesh):
    in_specs = (
        P(),
        P(),
        P("tm", None, "state", None),
        P("tm", None, None),
        P("tm", None, None),
        P("tm", None, None),
    )
    out_specs = (P("tm", None, "state"), P("tm", None))
    return jax.shard_map(shards, mesh=mesh, in_specs=in_specs, out_specs=out_specs, check_vma=False)
```

```python
import functools

import jax
import jax.numpy as jnp
from jax import lax
from jax.experimental import pallas as pl
from jax.experimental.pallas import tpu as pltpu
from jax.sharding import PartitionSpec as P

REACH = 3
TAPS = 2 * REACH + 1
PAD = 8
LEVELS = 4
LANES = 128
CHUNK = 64
VMEM_SPEC = pl.BlockSpec(memory_space=pltpu.VMEM)

FROM_LEFT, FROM_RIGHT, FAR_LEFT, FAR_RIGHT, AHEAD, FAR_AHEAD, FACTS = range(7)
TWIN = 7
KINDS = TWIN + 7


def prepare_kernel(offsets_ref, coefficients_ref, gain_ref, direct_ref, cells_ref, values_ref,
                   rows_ref, taps_ref, facts_ref):
    row_count, obs = rows_ref.shape
    first_row = lax.axis_index("state") * row_count
    cells = cells_ref[...]

    @pl.loop(0, row_count // CHUNK)
    def _(i):
        base = pl.multiple_of(i * CHUNK, CHUNK)
        ids = first_row + base + lax.broadcasted_iota(jnp.int32, (CHUNK, obs), 0)
        extra = jnp.where(ids == cells, direct_ref[...], 0.0)
        rows_ref[pl.ds(base, CHUNK), :] = (
            gain_ref[pl.ds(base, CHUNK), :].astype(jnp.float32) + extra
        ).astype(jnp.bfloat16)

    row = lax.broadcasted_iota(jnp.int32, facts_ref.shape, 0)
    facts_ref[...] = jnp.where(row == 0, cells.astype(jnp.float32), jnp.where(row == 1, values_ref[...], 0.0))

    coefficients = coefficients_ref[...]
    weights = coefficients / jnp.sum(coefficients, axis=0, keepdims=True)
    tap = lax.broadcasted_iota(jnp.int32, (8, coefficients.shape[1]), 0)
    dense = jnp.zeros((8, coefficients.shape[1]), jnp.float32)
    for t in range(coefficients.shape[0]):
        dense = dense + jnp.where(tap == offsets_ref[t] + REACH, weights[t : t + 1, :], 0.0)
    for b in range(coefficients.shape[1] // LANES):
        taps_ref[b * LANES : (b + 1) * LANES, :] = dense[:, b * LANES : (b + 1) * LANES].T


def spread_weights(taps_ref, wide_ref):
    @pl.loop(0, wide_ref.shape[1] // CHUNK)
    def _(i):
        rows = pl.ds(pl.multiple_of(i * CHUNK, CHUNK), CHUNK)
        block = taps_ref[rows, :]
        for j in range(TAPS):
            wide_ref[j, rows, :] = jnp.broadcast_to(block[:, j : j + 1], (CHUNK, LANES))


def start_panel(x_ref, first_column):
    groups, padded, _ = x_ref.shape
    cells = padded - 2 * PAD

    @pl.loop(0, padded // PAD)
    def _(i):
        row = i * PAD - PAD + lax.broadcasted_iota(jnp.int32, (PAD, LANES), 0)
        row = jnp.where(row < 0, row + cells, jnp.where(row >= cells, row - cells, row))
        column = first_column + lax.broadcasted_iota(jnp.int32, (PAD, LANES), 1)
        rows = pl.ds(pl.multiple_of(i * PAD, PAD), PAD)
        for g in range(groups - 1):
            x_ref[g, rows, :] = (row == column + g * LANES).astype(jnp.float32)
        x_ref[groups - 1, rows, :] = jnp.zeros((PAD, LANES), jnp.float32)


def spread(wide_ref, x_ref, y_ref, low_ref):
    groups, cells, _ = y_ref.shape

    @pl.loop(0, cells // CHUNK)
    def _(i):
        base = pl.multiple_of(i * CHUNK, CHUNK)
        rows = pl.ds(base, CHUNK)
        for g in range(groups):
            total = None
            for j in range(TAPS):
                part = wide_ref[j, rows, :] * x_ref[g, pl.ds(base + (PAD - REACH + j), CHUNK), :]
                total = part if total is None else total + part
            y_ref[g, rows, :] = total
            low_ref[rows, g * LANES : (g + 1) * LANES] = total.astype(jnp.bfloat16)


def mark(facts, hot_ref, forced_ref):
    obs, cells = hot_ref.shape
    columns = facts.T
    wanted = columns[:, 0:1].astype(jnp.int32)
    for b in range(cells // obs):
        ids = b * obs + lax.broadcasted_iota(jnp.int32, (obs, obs), 1)
        hot_ref[:, b * obs : (b + 1) * obs] = (ids == wanted).astype(jnp.bfloat16)
    lane = lax.broadcasted_iota(jnp.int32, (obs, LANES), 1)
    forced_ref[...] = jnp.where(lane == 0, -columns[:, 1:2], 0.0).astype(jnp.bfloat16)


def pick(hot_ref, forced_ref, low_ref, picked_ref):
    width = low_ref.shape[1]
    picked_ref[:, :width] = jnp.dot(
        hot_ref[...], low_ref[...], preferred_element_type=jnp.float32
    ).astype(jnp.bfloat16)
    picked_ref[:, width:] = forced_ref[...]


def correct(gains_ref, picked_ref, y_ref, store):
    groups = y_ref.shape[0]
    blocks, block, _ = gains_ref.shape

    @pl.loop(0, blocks)
    def _(i):
        base = pl.multiple_of(i * block, block)
        correction = jnp.dot(gains_ref[i], picked_ref[...], preferred_element_type=jnp.float32)
        for g in range(groups):
            value = y_ref[g, pl.ds(base, block), :] - correction[:, g * LANES : (g + 1) * LANES]
            if g == groups - 1:
                value = value - correction[:, groups * LANES :]
            store(g, base, block, value)


def scan_kernel(spans, ring, taps_ref, rows_ref, facts_ref, out_ref, offset_ref,
                gains, facts, wide_ref, x_ref, y_ref, low_ref, hot_ref, forced_ref, picked_ref,
                send_sem, recv_sem, local_sem):
    span, state = lax.axis_index("tm"), lax.axis_index("state")
    chip, core = state // 2, state % 2
    place = lambda step, which: lax.rem(chip + step, ring) * 2 + which
    right, left, far = (place(step, core) for step in (1, ring - 1, 2))
    twin = place(0, 1 - core)
    twin_of = lambda step: place(step, 1 - core)
    ahead, behind_span = lax.rem(span + 1, spans), lax.rem(span + spans - 1, spans)
    count = rows_ref.shape[0]
    near = count * 3 // 16
    whole, first, second, rest = (0, count), (0, near), (near, near), (2 * near, count - 2 * near)
    cells, groups = out_ref.shape[0], x_ref.shape[0]

    barrier = pltpu.get_barrier_semaphore()
    for there in ((span, right), (span, left), (span, twin), (ahead, state), (behind_span, state)):
        pl.semaphore_signal(barrier, inc=1, device_id=there, device_id_type=pl.DeviceIdType.MESH)
    pl.semaphore_wait(barrier, 5)

    def part(k, owner, rows):
        return gains.at[k, owner, pl.ds(*rows)]

    started = []

    def send(source, target, kind, k, there):
        copy = pltpu.make_async_remote_copy(
            src_ref=source, dst_ref=target, send_sem=send_sem.at[kind, k], recv_sem=recv_sem.at[kind, k],
            device_id=there, device_id_type=pl.DeviceIdType.MESH,
        )
        copy.start()
        started.append(copy)

    def arrive(target, kind, k):
        pltpu.make_async_remote_copy(
            src_ref=target, dst_ref=target, send_sem=send_sem.at[kind, k], recv_sem=recv_sem.at[kind, k],
            device_id=(span, twin), device_id_type=pl.DeviceIdType.MESH,
        ).wait_recv()

    def to_twin(k, owner, rows, kind):
        send(part(k, owner, rows), part(k, owner, rows), TWIN + kind, k, (span, twin))

    def go_ahead(k):
        source = rows_ref if k == 0 else part(k, state, whole)
        send(facts_ref if k == 0 else facts.at[k], facts.at[k + 1], FACTS, k + 1, (ahead, state))
        send(source, part(k + 1, state, whole), AHEAD, k + 1, (ahead, state))

    def go_round(k):
        source = rows_ref if k == 0 else part(k, state, whole)
        send(source, part(k, state, whole), FROM_LEFT, k, (span, right))
        send(source, part(k, state, whole), FROM_RIGHT, k, (span, left))
        send(source, part(k, state, whole), TWIN + AHEAD, k, (span, twin))

    def take_sides(k):
        across = (first, second) if k else ((0, count // 2), (count // 2, count // 2))
        arrive(part(k, left, whole), FROM_LEFT, k)
        send(part(k, left, across[0]), part(k, left, across[0]), FAR_LEFT, k, (span, right))
        to_twin(k, left, whole, FROM_LEFT)
        arrive(part(k, right, whole), FROM_RIGHT, k)
        send(part(k, right, across[1]), part(k, right, across[1]), FAR_RIGHT, k, (span, left))
        to_twin(k, right, whole, FROM_RIGHT)

    def take_far(k):
        across = (first, second) if k else ((0, count // 2), (count // 2, count // 2))
        for rows, kind in zip(across, (FAR_LEFT, FAR_RIGHT)):
            arrive(part(k, far, rows), kind, k)
            to_twin(k, far, rows, kind)

    def far_ahead(k):
        send(part(k, far, rest), part(k + 1, far, rest), FAR_AHEAD, k + 1, (ahead, state))

    def take_far_ahead(k):
        arrive(part(k, far, rest), FAR_AHEAD, k)
        if k < LEVELS - 1:
            far_ahead(k)
        to_twin(k, far, rest, FAR_AHEAD)

    def take_ahead(k):
        arrive(facts.at[k], FACTS, k)
        arrive(part(k, state, whole), AHEAD, k)

    def take_twin(k):
        across = (first, second) if k else ((0, count // 2), (count // 2, count // 2))
        arrive(part(k, twin, whole), TWIN + AHEAD, k)
        arrive(part(k, twin_of(ring - 1), whole), TWIN + FROM_LEFT, k)
        arrive(part(k, twin_of(1), whole), TWIN + FROM_RIGHT, k)
        for rows, kind in zip(across, (FAR_LEFT, FAR_RIGHT)):
            arrive(part(k, twin_of(2), rows), TWIN + kind, k)
        if k:
            arrive(part(k, twin_of(2), rest), TWIN + FAR_AHEAD, k)

    def keep(g, base, block, value):
        x_ref[g, pl.ds(base + PAD, block), :] = value

    def finish(g, base, block, value):
        if g < groups - 1:
            out_ref[pl.ds(base, block), g * LANES : (g + 1) * LANES] = value
        else:
            for piece in range(block // LANES):
                square = value[piece * LANES : (piece + 1) * LANES, :].T
                offset_ref[0:1, pl.ds(pl.multiple_of(base + piece * LANES, LANES), LANES)] = square[0:1, :]

    def look(k):
        def run():
            spread(wide_ref, x_ref, y_ref, low_ref)
            pick(hot_ref.at[k], forced_ref.at[k], low_ref, picked_ref)

        pl.when(span >= k)(run)

    def move(k):
        def run():
            correct(gains.at[k], picked_ref, y_ref, keep if k else finish)
            if k:
                for g in range(groups):
                    x_ref[g, 0:PAD, :] = x_ref[g, cells : cells + PAD, :]
                    x_ref[g, cells + PAD : cells + 2 * PAD, :] = x_ref[g, PAD : 2 * PAD, :]

        pl.when(span >= k)(run)

    def note(k):
        mark(facts_ref[...] if k == 0 else facts[k], hot_ref.at[k], forced_ref.at[k])

    go_ahead(0)
    go_round(0)
    own = pltpu.make_async_copy(rows_ref, gains.at[0, state], local_sem)
    own.start()
    spread_weights(taps_ref, wide_ref)
    start_panel(x_ref, state * out_ref.shape[1])
    take_ahead(1)
    go_ahead(1)
    take_sides(0)
    go_round(1)
    note(0)
    note(1)
    take_far(0)
    far_ahead(0)
    take_ahead(2)
    go_ahead(2)
    note(2)
    take_sides(1)
    take_ahead(3)
    go_round(3)
    note(3)
    take_far_ahead(1)
    take_far(1)
    look(3)
    take_sides(3)
    go_round(2)
    take_far_ahead(2)
    take_far_ahead(3)
    take_far(3)
    take_twin(3)
    move(3)
    take_sides(2)
    look(2)
    take_far(2)
    take_twin(2)
    move(2)
    look(1)
    take_twin(1)
    move(1)
    look(0)
    own.wait()
    take_twin(0)
    move(0)
    for copy in started:
        copy.wait_send()


def shards(spans, states, offsets, coefficients, gain_matrix, direct_gain, observed_cells, observed_values):
    row_count, obs = gain_matrix.shape[2:]
    cells = coefficients.shape[1]
    rows, taps, facts = pl.pallas_call(
        prepare_kernel,
        out_shape=(
            jax.ShapeDtypeStruct((row_count, obs), jnp.bfloat16),
            jax.ShapeDtypeStruct((cells, 8), jnp.float32),
            jax.ShapeDtypeStruct((8, obs), jnp.float32),
        ),
        in_specs=[pl.BlockSpec(memory_space=pltpu.SMEM)] + [VMEM_SPEC] * 5,
        out_specs=(VMEM_SPEC,) * 3,
        name="prepare",
    )(offsets, coefficients, gain_matrix[0, 0], direct_gain[0], observed_cells[0], observed_values[0])
    groups = row_count // LANES + 1
    out, offset = pl.pallas_call(
        functools.partial(scan_kernel, spans, states // 2),
        out_shape=(
            jax.ShapeDtypeStruct((cells, row_count), jnp.float32),
            jax.ShapeDtypeStruct((1, cells), jnp.float32),
        ),
        in_specs=[VMEM_SPEC] * 3,
        out_specs=(VMEM_SPEC, VMEM_SPEC),
        scratch_shapes=[
            pltpu.VMEM((LEVELS, states, row_count, obs), jnp.bfloat16),
            pltpu.VMEM((LEVELS, 8, obs), jnp.float32),
            pltpu.VMEM((TAPS, cells, LANES), jnp.float32),
            pltpu.VMEM((groups, cells + 2 * PAD, LANES), jnp.float32),
            pltpu.VMEM((groups, cells, LANES), jnp.float32),
            pltpu.VMEM((cells, groups * LANES), jnp.bfloat16),
            pltpu.VMEM((LEVELS, obs, cells), jnp.bfloat16),
            pltpu.VMEM((LEVELS, obs, LANES), jnp.bfloat16),
            pltpu.VMEM((obs, (groups + 1) * LANES), jnp.bfloat16),
            pltpu.SemaphoreType.DMA((KINDS, LEVELS)),
            pltpu.SemaphoreType.DMA((KINDS, LEVELS)),
            pltpu.SemaphoreType.DMA,
        ],
        compiler_params=pltpu.CompilerParams(
            collective_id=0, has_side_effects=True, vmem_limit_bytes=56 * 1024 * 1024
        ),
        name="scan",
    )(taps, rows, facts)
    return out[None], offset


def solution(mesh):
    in_specs = (
        P(),
        P(),
        P("tm", None, "state", None),
        P("tm", None, None),
        P("tm", None, None),
        P("tm", None, None),
    )
    out_specs = (P("tm", None, "state"), P("tm", None))
    run = functools.partial(shards, mesh.shape["tm"], mesh.shape["state"])
    return jax.shard_map(run, mesh=mesh, in_specs=in_specs, out_specs=out_specs, check_vma=False)
```

```python
import functools

import jax
import jax.numpy as jnp
from jax import lax
from jax.experimental import pallas as pl
from jax.experimental.pallas import tpu as pltpu
from jax.sharding import PartitionSpec as P

REACH = 3
TAPS = 2 * REACH + 1
PAD = 8
LEVELS = 4
LANES = 128
CHUNK = 64
VMEM_SPEC = pl.BlockSpec(memory_space=pltpu.VMEM)

FROM_LEFT, FROM_RIGHT, FAR_LEFT, FAR_RIGHT, AHEAD, AHEAD_LATE, FACTS = range(7)
TWIN = 7
KINDS = TWIN + 7


def prepare_kernel(offsets_ref, coefficients_ref, gain_ref, direct_ref, cells_ref, values_ref,
                   rows_ref, taps_ref, facts_ref):
    row_count, obs = rows_ref.shape
    first_row = lax.axis_index("state") * row_count
    cells = cells_ref[...]

    @pl.loop(0, row_count // CHUNK)
    def _(i):
        base = pl.multiple_of(i * CHUNK, CHUNK)
        ids = first_row + base + lax.broadcasted_iota(jnp.int32, (CHUNK, obs), 0)
        extra = jnp.where(ids == cells, direct_ref[...], 0.0)
        rows_ref[pl.ds(base, CHUNK), :] = (
            gain_ref[pl.ds(base, CHUNK), :].astype(jnp.float32) + extra
        ).astype(jnp.bfloat16)

    row = lax.broadcasted_iota(jnp.int32, facts_ref.shape, 0)
    facts_ref[...] = jnp.where(row == 0, cells.astype(jnp.float32), jnp.where(row == 1, values_ref[...], 0.0))

    coefficients = coefficients_ref[...]
    weights = coefficients / jnp.sum(coefficients, axis=0, keepdims=True)
    tap = lax.broadcasted_iota(jnp.int32, (8, coefficients.shape[1]), 0)
    dense = jnp.zeros((8, coefficients.shape[1]), jnp.float32)
    for t in range(coefficients.shape[0]):
        dense = dense + jnp.where(tap == offsets_ref[t] + REACH, weights[t : t + 1, :], 0.0)
    for b in range(coefficients.shape[1] // LANES):
        taps_ref[b * LANES : (b + 1) * LANES, :] = dense[:, b * LANES : (b + 1) * LANES].T


def spread_weights(taps_ref, wide_ref):
    @pl.loop(0, wide_ref.shape[1] // CHUNK)
    def _(i):
        rows = pl.ds(pl.multiple_of(i * CHUNK, CHUNK), CHUNK)
        block = taps_ref[rows, :]
        for j in range(TAPS):
            wide_ref[j, rows, :] = jnp.broadcast_to(block[:, j : j + 1], (CHUNK, LANES))


def start_panel(x_ref, first_column):
    groups, padded, _ = x_ref.shape
    cells = padded - 2 * PAD

    @pl.loop(0, padded // PAD)
    def _(i):
        row = i * PAD - PAD + lax.broadcasted_iota(jnp.int32, (PAD, LANES), 0)
        row = jnp.where(row < 0, row + cells, jnp.where(row >= cells, row - cells, row))
        column = first_column + lax.broadcasted_iota(jnp.int32, (PAD, LANES), 1)
        rows = pl.ds(pl.multiple_of(i * PAD, PAD), PAD)
        for g in range(groups - 1):
            x_ref[g, rows, :] = (row == column + g * LANES).astype(jnp.float32)
        x_ref[groups - 1, rows, :] = jnp.zeros((PAD, LANES), jnp.float32)


def spread(wide_ref, x_ref, y_ref, low_ref):
    groups, cells, _ = y_ref.shape

    @pl.loop(0, cells // CHUNK)
    def _(i):
        base = pl.multiple_of(i * CHUNK, CHUNK)
        rows = pl.ds(base, CHUNK)
        for g in range(groups):
            total = None
            for j in range(TAPS):
                part = wide_ref[j, rows, :] * x_ref[g, pl.ds(base + (PAD - REACH + j), CHUNK), :]
                total = part if total is None else total + part
            y_ref[g, rows, :] = total
            low_ref[rows, g * LANES : (g + 1) * LANES] = total.astype(jnp.bfloat16)


def mark(facts, hot_ref, forced_ref):
    obs, cells = hot_ref.shape
    columns = facts.T
    wanted = columns[:, 0:1].astype(jnp.int32)
    for b in range(cells // obs):
        ids = b * obs + lax.broadcasted_iota(jnp.int32, (obs, obs), 1)
        hot_ref[:, b * obs : (b + 1) * obs] = (ids == wanted).astype(jnp.bfloat16)
    lane = lax.broadcasted_iota(jnp.int32, (obs, LANES), 1)
    forced_ref[...] = jnp.where(lane == 0, -columns[:, 1:2], 0.0).astype(jnp.bfloat16)


def pick(hot_ref, forced_ref, low_ref, picked_ref):
    width = low_ref.shape[1]
    picked_ref[:, :width] = jnp.dot(
        hot_ref[...], low_ref[...], preferred_element_type=jnp.float32
    ).astype(jnp.bfloat16)
    picked_ref[:, width:] = forced_ref[...]


def correct(gains_ref, picked_ref, y_ref, store):
    groups = y_ref.shape[0]
    blocks, block, _ = gains_ref.shape

    @pl.loop(0, blocks)
    def _(i):
        base = pl.multiple_of(i * block, block)
        correction = jnp.dot(gains_ref[i], picked_ref[...], preferred_element_type=jnp.float32)
        for g in range(groups):
            value = y_ref[g, pl.ds(base, block), :] - correction[:, g * LANES : (g + 1) * LANES]
            if g == groups - 1:
                value = value - correction[:, groups * LANES :]
            store(g, base, block, value)


def scan_kernel(spans, ring, taps_ref, rows_ref, facts_ref, out_ref, offset_ref,
                gains, facts, wide_ref, x_ref, y_ref, low_ref, hot_ref, forced_ref, picked_ref,
                send_sem, recv_sem, local_sem):
    span, state = lax.axis_index("tm"), lax.axis_index("state")
    chip, core = state // 2, state % 2
    place = lambda step, which: lax.rem(chip + step, ring) * 2 + which
    right, left, far = (place(step, core) for step in (1, ring - 1, 2))
    twin = place(0, 1 - core)
    twin_of = lambda step: place(step, 1 - core)
    ahead, behind_span = lax.rem(span + 1, spans), lax.rem(span + spans - 1, spans)
    count = rows_ref.shape[0]
    half = count // 2
    whole, halves = (0, count), ((0, half), (half, half))
    cells, groups = out_ref.shape[0], x_ref.shape[0]

    barrier = pltpu.get_barrier_semaphore()
    for there in ((span, right), (span, left), (span, twin), (ahead, state), (behind_span, state)):
        pl.semaphore_signal(barrier, inc=1, device_id=there, device_id_type=pl.DeviceIdType.MESH)
    pl.semaphore_wait(barrier, 5)

    def part(k, owner, rows):
        return gains.at[k, owner, pl.ds(*rows)]

    started = []

    def send(source, target, kind, k, there):
        copy = pltpu.make_async_remote_copy(
            src_ref=source, dst_ref=target, send_sem=send_sem.at[kind, k], recv_sem=recv_sem.at[kind, k],
            device_id=there, device_id_type=pl.DeviceIdType.MESH,
        )
        copy.start()
        started.append(copy)

    def arrive(target, kind, k):
        pltpu.make_async_remote_copy(
            src_ref=target, dst_ref=target, send_sem=send_sem.at[kind, k], recv_sem=recv_sem.at[kind, k],
            device_id=(span, twin), device_id_type=pl.DeviceIdType.MESH,
        ).wait_recv()

    def to_twin(k, owner, rows, kind):
        send(part(k, owner, rows), part(k, owner, rows), TWIN + kind, k, (span, twin))

    def go_ahead(k, h):
        rows = halves[h]
        source = rows_ref.at[pl.ds(*rows)] if k == 0 else part(k, state, rows)
        if h == 0:
            send(facts_ref if k == 0 else facts.at[k], facts.at[k + 1], FACTS, k + 1, (ahead, state))
        send(source, part(k + 1, state, rows), AHEAD + h, k + 1, (ahead, state))

    def take_ahead(k, h):
        if h == 0:
            arrive(facts.at[k], FACTS, k)
        arrive(part(k, state, halves[h]), AHEAD + h, k)
        if k < LEVELS - 1:
            go_ahead(k, h)

    def go_round(k):
        source = rows_ref if k == 0 else part(k, state, whole)
        send(source, part(k, state, whole), FROM_LEFT, k, (span, right))
        send(source, part(k, state, whole), FROM_RIGHT, k, (span, left))
        send(source, part(k, state, whole), TWIN + AHEAD, k, (span, twin))

    def take_sides(k):
        for owner, kind in ((left, FROM_LEFT), (right, FROM_RIGHT)):
            arrive(part(k, owner, whole), kind, k)
            to_twin(k, owner, whole, kind)

    def relay(k):
        send(part(k, left, halves[0]), part(k, left, halves[0]), FAR_LEFT, k, (span, right))
        send(part(k, right, halves[1]), part(k, right, halves[1]), FAR_RIGHT, k, (span, left))

    def take_far(k):
        for rows, kind in zip(halves, (FAR_LEFT, FAR_RIGHT)):
            arrive(part(k, far, rows), kind, k)
            to_twin(k, far, rows, kind)

    def take_twin(k):
        arrive(part(k, twin, whole), TWIN + AHEAD, k)
        arrive(part(k, twin_of(ring - 1), whole), TWIN + FROM_LEFT, k)
        arrive(part(k, twin_of(1), whole), TWIN + FROM_RIGHT, k)
        for rows, kind in zip(halves, (FAR_LEFT, FAR_RIGHT)):
            arrive(part(k, twin_of(2), rows), TWIN + kind, k)

    def keep(g, base, block, value):
        x_ref[g, pl.ds(base + PAD, block), :] = value

    def finish(g, base, block, value):
        if g < groups - 1:
            out_ref[pl.ds(base, block), g * LANES : (g + 1) * LANES] = value
        else:
            for piece in range(block // LANES):
                square = value[piece * LANES : (piece + 1) * LANES, :].T
                offset_ref[0:1, pl.ds(pl.multiple_of(base + piece * LANES, LANES), LANES)] = square[0:1, :]

    def look(k):
        def run():
            spread(wide_ref, x_ref, y_ref, low_ref)
            pick(hot_ref.at[k], forced_ref.at[k], low_ref, picked_ref)

        pl.when(span >= k)(run)

    def move(k):
        def run():
            correct(gains.at[k], picked_ref, y_ref, keep if k else finish)
            if k:
                for g in range(groups):
                    x_ref[g, 0:PAD, :] = x_ref[g, cells : cells + PAD, :]
                    x_ref[g, cells + PAD : cells + 2 * PAD, :] = x_ref[g, PAD : 2 * PAD, :]

        pl.when(span >= k)(run)

    def note(k):
        mark(facts_ref[...] if k == 0 else facts[k], hot_ref.at[k], forced_ref.at[k])

    go_ahead(0, 0)
    go_ahead(0, 1)
    go_round(0)
    own = pltpu.make_async_copy(rows_ref, gains.at[0, state], local_sem)
    own.start()
    spread_weights(taps_ref, wide_ref)
    take_ahead(1, 0)
    start_panel(x_ref, state * out_ref.shape[1])
    note(0)
    take_ahead(1, 1)
    go_round(1)
    take_sides(0)
    note(1)
    take_ahead(2, 0)
    note(2)
    take_ahead(2, 1)
    go_round(2)
    take_sides(1)
    take_ahead(3, 0)
    note(3)
    take_ahead(3, 1)
    go_round(3)
    take_sides(2)
    relay(2)
    look(3)
    take_sides(3)
    relay(3)
    relay(1)
    relay(0)
    take_far(2)
    take_far(3)
    take_twin(3)
    move(3)
    take_far(1)
    look(2)
    take_twin(2)
    move(2)
    take_far(0)
    look(1)
    take_twin(1)
    move(1)
    look(0)
    own.wait()
    take_twin(0)
    move(0)
    for copy in started:
        copy.wait_send()


def shards(spans, states, offsets, coefficients, gain_matrix, direct_gain, observed_cells, observed_values):
    row_count, obs = gain_matrix.shape[2:]
    cells = coefficients.shape[1]
    rows, taps, facts = pl.pallas_call(
        prepare_kernel,
        out_shape=(
            jax.ShapeDtypeStruct((row_count, obs), jnp.bfloat16),
            jax.ShapeDtypeStruct((cells, 8), jnp.float32),
            jax.ShapeDtypeStruct((8, obs), jnp.float32),
        ),
        in_specs=[pl.BlockSpec(memory_space=pltpu.SMEM)] + [VMEM_SPEC] * 5,
        out_specs=(VMEM_SPEC,) * 3,
        name="prepare",
    )(offsets, coefficients, gain_matrix[0, 0], direct_gain[0], observed_cells[0], observed_values[0])
    groups = row_count // LANES + 1
    out, offset = pl.pallas_call(
        functools.partial(scan_kernel, spans, states // 2),
        out_shape=(
            jax.ShapeDtypeStruct((cells, row_count), jnp.float32),
            jax.ShapeDtypeStruct((1, cells), jnp.float32),
        ),
        in_specs=[VMEM_SPEC] * 3,
        out_specs=(VMEM_SPEC, VMEM_SPEC),
        scratch_shapes=[
            pltpu.VMEM((LEVELS, states, row_count, obs), jnp.bfloat16),
            pltpu.VMEM((LEVELS, 8, obs), jnp.float32),
            pltpu.VMEM((TAPS, cells, LANES), jnp.float32),
            pltpu.VMEM((groups, cells + 2 * PAD, LANES), jnp.float32),
            pltpu.VMEM((groups, cells, LANES), jnp.float32),
            pltpu.VMEM((cells, groups * LANES), jnp.bfloat16),
            pltpu.VMEM((LEVELS, obs, cells), jnp.bfloat16),
            pltpu.VMEM((LEVELS, obs, LANES), jnp.bfloat16),
            pltpu.VMEM((obs, (groups + 1) * LANES), jnp.bfloat16),
            pltpu.SemaphoreType.DMA((KINDS, LEVELS)),
            pltpu.SemaphoreType.DMA((KINDS, LEVELS)),
            pltpu.SemaphoreType.DMA,
        ],
        compiler_params=pltpu.CompilerParams(
            collective_id=0, has_side_effects=True, vmem_limit_bytes=56 * 1024 * 1024
        ),
        name="scan",
    )(taps, rows, facts)
    return out[None], offset


def solution(mesh):
    in_specs = (
        P(),
        P(),
        P("tm", None, "state", None),
        P("tm", None, None),
        P("tm", None, None),
        P("tm", None, None),
    )
    out_specs = (P("tm", None, "state"), P("tm", None))
    run = functools.partial(shards, mesh.shape["tm"], mesh.shape["state"])
    return jax.shard_map(run, mesh=mesh, in_specs=in_specs, out_specs=out_specs, check_vma=False)
```

```python
import functools

import jax
import jax.numpy as jnp
from jax import lax
from jax.experimental import pallas as pl
from jax.experimental.pallas import tpu as pltpu
from jax.sharding import PartitionSpec as P

REACH = 3
TAPS = 2 * REACH + 1
PAD = 8
LEVELS = 4
LANES = 128
CHUNK = 64
VMEM_SPEC = pl.BlockSpec(memory_space=pltpu.VMEM)

FROM_LEFT, FROM_RIGHT, FAR_LEFT, FAR_RIGHT, AHEAD, AHEAD_LATE, FACTS = range(7)
TWIN = 7
KINDS = TWIN + 7


def prepare_kernel(offsets_ref, coefficients_ref, gain_ref, direct_ref, cells_ref, values_ref,
                   rows_ref, taps_ref, facts_ref):
    row_count, obs = rows_ref.shape
    first_row = lax.axis_index("state") * row_count
    cells = cells_ref[...]

    @pl.loop(0, row_count // CHUNK)
    def _(i):
        base = pl.multiple_of(i * CHUNK, CHUNK)
        ids = first_row + base + lax.broadcasted_iota(jnp.int32, (CHUNK, obs), 0)
        extra = jnp.where(ids == cells, direct_ref[...], 0.0)
        rows_ref[pl.ds(base, CHUNK), :] = (
            gain_ref[pl.ds(base, CHUNK), :].astype(jnp.float32) + extra
        ).astype(jnp.bfloat16)

    row = lax.broadcasted_iota(jnp.int32, facts_ref.shape, 0)
    facts_ref[...] = jnp.where(row == 0, cells.astype(jnp.float32), jnp.where(row == 1, values_ref[...], 0.0))

    coefficients = coefficients_ref[...]
    weights = coefficients / jnp.sum(coefficients, axis=0, keepdims=True)
    tap = lax.broadcasted_iota(jnp.int32, (8, coefficients.shape[1]), 0)
    dense = jnp.zeros((8, coefficients.shape[1]), jnp.float32)
    for t in range(coefficients.shape[0]):
        dense = dense + jnp.where(tap == offsets_ref[t] + REACH, weights[t : t + 1, :], 0.0)
    for b in range(coefficients.shape[1] // LANES):
        taps_ref[b * LANES : (b + 1) * LANES, :] = dense[:, b * LANES : (b + 1) * LANES].T


def spread_weights(quarter, taps_ref, wide_ref):
    chunks = wide_ref.shape[1] // CHUNK // 4

    @pl.loop(quarter * chunks, (quarter + 1) * chunks)
    def _(i):
        rows = pl.ds(pl.multiple_of(i * CHUNK, CHUNK), CHUNK)
        block = taps_ref[rows, :]
        for j in range(TAPS):
            wide_ref[j, rows, :] = jnp.broadcast_to(block[:, j : j + 1], (CHUNK, LANES))


def start_panel(x_ref, first_column):
    groups, padded, _ = x_ref.shape
    cells = padded - 2 * PAD

    @pl.loop(0, padded // PAD)
    def _(i):
        row = i * PAD - PAD + lax.broadcasted_iota(jnp.int32, (PAD, LANES), 0)
        row = jnp.where(row < 0, row + cells, jnp.where(row >= cells, row - cells, row))
        column = first_column + lax.broadcasted_iota(jnp.int32, (PAD, LANES), 1)
        rows = pl.ds(pl.multiple_of(i * PAD, PAD), PAD)
        for g in range(groups - 1):
            x_ref[g, rows, :] = (row == column + g * LANES).astype(jnp.float32)
        x_ref[groups - 1, rows, :] = jnp.zeros((PAD, LANES), jnp.float32)


def spread(wide_ref, x_ref, y_ref, low_ref):
    groups, cells, _ = y_ref.shape

    @pl.loop(0, cells // CHUNK)
    def _(i):
        base = pl.multiple_of(i * CHUNK, CHUNK)
        rows = pl.ds(base, CHUNK)
        for g in range(groups):
            total = None
            for j in range(TAPS):
                part = wide_ref[j, rows, :] * x_ref[g, pl.ds(base + (PAD - REACH + j), CHUNK), :]
                total = part if total is None else total + part
            y_ref[g, rows, :] = total
            low_ref[rows, g * LANES : (g + 1) * LANES] = total.astype(jnp.bfloat16)


def mark(facts, hot_ref, forced_ref):
    obs, cells = hot_ref.shape
    columns = facts.T
    wanted = columns[:, 0:1].astype(jnp.int32)
    for b in range(cells // obs):
        ids = b * obs + lax.broadcasted_iota(jnp.int32, (obs, obs), 1)
        hot_ref[:, b * obs : (b + 1) * obs] = (ids == wanted).astype(jnp.bfloat16)
    lane = lax.broadcasted_iota(jnp.int32, (obs, LANES), 1)
    forced_ref[...] = jnp.where(lane == 0, -columns[:, 1:2], 0.0).astype(jnp.bfloat16)


def pick(hot_ref, forced_ref, low_ref, picked_ref):
    width = low_ref.shape[1]
    picked_ref[:, :width] = jnp.dot(
        hot_ref[...], low_ref[...], preferred_element_type=jnp.float32
    ).astype(jnp.bfloat16)
    picked_ref[:, width:] = forced_ref[...]


def correct(gains_ref, picked_ref, y_ref, store):
    groups = y_ref.shape[0]
    blocks, block, _ = gains_ref.shape

    @pl.loop(0, blocks)
    def _(i):
        base = pl.multiple_of(i * block, block)
        correction = jnp.dot(gains_ref[i], picked_ref[...], preferred_element_type=jnp.float32)
        for g in range(groups):
            value = y_ref[g, pl.ds(base, block), :] - correction[:, g * LANES : (g + 1) * LANES]
            if g == groups - 1:
                value = value - correction[:, groups * LANES :]
            store(g, base, block, value)


def scan_kernel(spans, ring, taps_ref, rows_ref, facts_ref, out_ref, offset_ref,
                gains, facts, wide_ref, x_ref, y_ref, low_ref, hot_ref, forced_ref, picked_ref,
                send_sem, recv_sem, local_sem):
    span, state = lax.axis_index("tm"), lax.axis_index("state")
    chip, core = state // 2, state % 2
    place = lambda step, which: lax.rem(chip + step, ring) * 2 + which
    right, left, far = (place(step, core) for step in (1, ring - 1, 2))
    twin = place(0, 1 - core)
    twin_of = lambda step: place(step, 1 - core)
    ahead, behind_span = lax.rem(span + 1, spans), lax.rem(span + spans - 1, spans)
    count = rows_ref.shape[0]
    half = count // 2
    whole, halves = (0, count), ((0, half), (half, half))
    cells, groups = out_ref.shape[0], x_ref.shape[0]

    barrier = pltpu.get_barrier_semaphore()
    for there in ((span, right), (span, left), (span, twin), (ahead, state), (behind_span, state)):
        pl.semaphore_signal(barrier, inc=1, device_id=there, device_id_type=pl.DeviceIdType.MESH)
    pl.semaphore_wait(barrier, 5)

    def part(k, owner, rows):
        return gains.at[k, owner, pl.ds(*rows)]

    started = []

    def send(source, target, kind, k, there):
        copy = pltpu.make_async_remote_copy(
            src_ref=source, dst_ref=target, send_sem=send_sem.at[kind, k], recv_sem=recv_sem.at[kind, k],
            device_id=there, device_id_type=pl.DeviceIdType.MESH,
        )
        copy.start()
        started.append(copy)

    def arrive(target, kind, k):
        pltpu.make_async_remote_copy(
            src_ref=target, dst_ref=target, send_sem=send_sem.at[kind, k], recv_sem=recv_sem.at[kind, k],
            device_id=(span, twin), device_id_type=pl.DeviceIdType.MESH,
        ).wait_recv()

    def to_twin(k, owner, rows, kind):
        send(part(k, owner, rows), part(k, owner, rows), TWIN + kind, k, (span, twin))

    def go_ahead(k, h):
        rows = halves[h]
        source = rows_ref.at[pl.ds(*rows)] if k == 0 else part(k, state, rows)
        if h == 0:
            send(facts_ref if k == 0 else facts.at[k], facts.at[k + 1], FACTS, k + 1, (ahead, state))
        send(source, part(k + 1, state, rows), AHEAD + h, k + 1, (ahead, state))

    def take_ahead(k, h):
        if h == 0:
            arrive(facts.at[k], FACTS, k)
        arrive(part(k, state, halves[h]), AHEAD + h, k)
        if k < LEVELS - 1:
            go_ahead(k, h)

    def go_round(k):
        source = rows_ref if k == 0 else part(k, state, whole)
        send(source, part(k, state, whole), FROM_LEFT, k, (span, right))
        send(source, part(k, state, whole), FROM_RIGHT, k, (span, left))
        send(source, part(k, state, whole), TWIN + AHEAD, k, (span, twin))

    def take_sides(k):
        for owner, kind in ((left, FROM_LEFT), (right, FROM_RIGHT)):
            arrive(part(k, owner, whole), kind, k)
            to_twin(k, owner, whole, kind)

    def relay(k):
        send(part(k, left, halves[0]), part(k, left, halves[0]), FAR_LEFT, k, (span, right))
        send(part(k, right, halves[1]), part(k, right, halves[1]), FAR_RIGHT, k, (span, left))

    def take_far(k):
        for rows, kind in zip(halves, (FAR_LEFT, FAR_RIGHT)):
            arrive(part(k, far, rows), kind, k)
            to_twin(k, far, rows, kind)

    def take_twin(k):
        arrive(part(k, twin, whole), TWIN + AHEAD, k)
        arrive(part(k, twin_of(ring - 1), whole), TWIN + FROM_LEFT, k)
        arrive(part(k, twin_of(1), whole), TWIN + FROM_RIGHT, k)
        for rows, kind in zip(halves, (FAR_LEFT, FAR_RIGHT)):
            arrive(part(k, twin_of(2), rows), TWIN + kind, k)

    def keep(g, base, block, value):
        x_ref[g, pl.ds(base + PAD, block), :] = value

    def finish(g, base, block, value):
        if g < groups - 1:
            out_ref[pl.ds(base, block), g * LANES : (g + 1) * LANES] = value
        else:
            for piece in range(block // LANES):
                square = value[piece * LANES : (piece + 1) * LANES, :].T
                offset_ref[0:1, pl.ds(pl.multiple_of(base + piece * LANES, LANES), LANES)] = square[0:1, :]

    def look(k):
        def run():
            spread(wide_ref, x_ref, y_ref, low_ref)
            pick(hot_ref.at[k], forced_ref.at[k], low_ref, picked_ref)

        pl.when(span >= k)(run)

    def move(k):
        def run():
            correct(gains.at[k], picked_ref, y_ref, keep if k else finish)
            if k:
                for g in range(groups):
                    x_ref[g, 0:PAD, :] = x_ref[g, cells : cells + PAD, :]
                    x_ref[g, cells + PAD : cells + 2 * PAD, :] = x_ref[g, PAD : 2 * PAD, :]

        pl.when(span >= k)(run)

    def note(k):
        mark(facts_ref[...] if k == 0 else facts[k], hot_ref.at[k], forced_ref.at[k])

    def widen(quarter):
        spread_weights(quarter, taps_ref, wide_ref)

    go_ahead(0, 0)
    go_ahead(0, 1)
    go_round(0)
    own = pltpu.make_async_copy(rows_ref, gains.at[0, state], local_sem)
    own.start()
    start_panel(x_ref, state * out_ref.shape[1])
    note(0)
    widen(0)
    take_ahead(1, 0)
    widen(1)
    take_ahead(1, 1)
    go_round(1)
    take_sides(0)
    note(1)
    take_ahead(2, 0)
    widen(2)
    take_ahead(2, 1)
    go_round(2)
    note(2)
    take_sides(1)
    take_ahead(3, 0)
    widen(3)
    take_ahead(3, 1)
    go_round(3)
    note(3)
    take_sides(2)
    look(3)
    take_sides(3)
    relay(3)
    relay(2)
    relay(1)
    relay(0)
    take_far(3)
    take_twin(3)
    move(3)
    take_far(2)
    look(2)
    take_twin(2)
    move(2)
    take_far(1)
    take_far(0)
    look(1)
    take_twin(1)
    move(1)
    look(0)
    own.wait()
    take_twin(0)
    move(0)
    for copy in started:
        copy.wait_send()


def deliver_kernel(out_ref, offset_ref, out_final_ref, offset_final_ref, block_ref, line_ref, in_sem, done_sem):
    blocks, rows, _ = block_ref.shape
    pieces = [
        (out_ref.at[pl.ds(b * rows, rows)], block_ref.at[b], out_final_ref.at[pl.ds(b * rows, rows)])
        for b in range(blocks)
    ] + [(offset_ref, line_ref, offset_final_ref)]
    taken = [pltpu.make_async_copy(a, b, in_sem.at[n]) for n, (a, b, _) in enumerate(pieces)]
    given = [pltpu.make_async_copy(b, c, done_sem.at[n]) for n, (_, b, c) in enumerate(pieces)]
    for copy in taken:
        copy.start()
    for before, after in zip(taken, given):
        before.wait()
        after.start()
    for copy in given:
        copy.wait()


def shards(spans, states, offsets, coefficients, gain_matrix, direct_gain, observed_cells, observed_values):
    row_count, obs = gain_matrix.shape[2:]
    cells = coefficients.shape[1]
    rows, taps, facts = pl.pallas_call(
        prepare_kernel,
        out_shape=(
            jax.ShapeDtypeStruct((row_count, obs), jnp.bfloat16),
            jax.ShapeDtypeStruct((cells, 8), jnp.float32),
            jax.ShapeDtypeStruct((8, obs), jnp.float32),
        ),
        in_specs=[pl.BlockSpec(memory_space=pltpu.SMEM)] + [VMEM_SPEC] * 5,
        out_specs=(VMEM_SPEC,) * 3,
        name="prepare",
    )(offsets, coefficients, gain_matrix[0, 0], direct_gain[0], observed_cells[0], observed_values[0])
    groups = row_count // LANES + 1
    out, offset = pl.pallas_call(
        functools.partial(scan_kernel, spans, states // 2),
        out_shape=(
            jax.ShapeDtypeStruct((cells, row_count), jnp.float32),
            jax.ShapeDtypeStruct((1, cells), jnp.float32),
        ),
        in_specs=[VMEM_SPEC] * 3,
        out_specs=(VMEM_SPEC, VMEM_SPEC),
        scratch_shapes=[
            pltpu.VMEM((LEVELS, states, row_count, obs), jnp.bfloat16),
            pltpu.VMEM((LEVELS, 8, obs), jnp.float32),
            pltpu.VMEM((TAPS, cells, LANES), jnp.float32),
            pltpu.VMEM((groups, cells + 2 * PAD, LANES), jnp.float32),
            pltpu.VMEM((groups, cells, LANES), jnp.float32),
            pltpu.VMEM((cells, groups * LANES), jnp.bfloat16),
            pltpu.VMEM((LEVELS, obs, cells), jnp.bfloat16),
            pltpu.VMEM((LEVELS, obs, LANES), jnp.bfloat16),
            pltpu.VMEM((obs, (groups + 1) * LANES), jnp.bfloat16),
            pltpu.SemaphoreType.DMA((KINDS, LEVELS)),
            pltpu.SemaphoreType.DMA((KINDS, LEVELS)),
            pltpu.SemaphoreType.DMA,
        ],
        compiler_params=pltpu.CompilerParams(
            collective_id=0, has_side_effects=True, vmem_limit_bytes=56 * 1024 * 1024
        ),
        name="scan",
    )(taps, rows, facts)
    anywhere = pl.BlockSpec(memory_space=pl.ANY)
    blocks = 8
    out, offset = pl.pallas_call(
        deliver_kernel,
        out_shape=(
            jax.ShapeDtypeStruct(out.shape, out.dtype),
            jax.ShapeDtypeStruct(offset.shape, offset.dtype),
        ),
        in_specs=[anywhere] * 2,
        out_specs=(anywhere,) * 2,
        scratch_shapes=[
            pltpu.VMEM((blocks, cells // blocks, row_count), jnp.float32),
            pltpu.VMEM(offset.shape, jnp.float32),
            pltpu.SemaphoreType.DMA((blocks + 1,)),
            pltpu.SemaphoreType.DMA((blocks + 1,)),
        ],
        name="deliver",
    )(out, offset)
    return out[None], offset


def solution(mesh):
    in_specs = (
        P(),
        P(),
        P("tm", None, "state", None),
        P("tm", None, None),
        P("tm", None, None),
        P("tm", None, None),
    )
    out_specs = (P("tm", None, "state"), P("tm", None))
    run = functools.partial(shards, mesh.shape["tm"], mesh.shape["state"])
    return jax.shard_map(run, mesh=mesh, in_specs=in_specs, out_specs=out_specs, check_vma=False)
```

```python
import functools

import jax
import jax.numpy as jnp
from jax import lax
from jax.experimental import pallas as pl
from jax.experimental.pallas import tpu as pltpu
from jax.sharding import PartitionSpec as P

REACH = 3
TAPS = 2 * REACH + 1
PAD = 8
LEVELS = 4
LANES = 128
CHUNK = 64
VMEM_SPEC = pl.BlockSpec(memory_space=pltpu.VMEM)

FROM_LEFT, FROM_RIGHT, FAR_LEFT, FAR_RIGHT, AHEAD, AHEAD_LATE, FACTS, FAR_AHEAD = range(8)
TWIN = 8
KINDS = TWIN + 8


def prepare_kernel(offsets_ref, coefficients_ref, gain_ref, direct_ref, cells_ref, values_ref,
                   rows_ref, taps_ref, facts_ref):
    row_count, obs = rows_ref.shape
    first_row = lax.axis_index("state") * row_count
    cells = cells_ref[...]

    @pl.loop(0, row_count // CHUNK)
    def _(i):
        base = pl.multiple_of(i * CHUNK, CHUNK)
        ids = first_row + base + lax.broadcasted_iota(jnp.int32, (CHUNK, obs), 0)
        extra = jnp.where(ids == cells, direct_ref[...], 0.0)
        rows_ref[pl.ds(base, CHUNK), :] = (
            gain_ref[pl.ds(base, CHUNK), :].astype(jnp.float32) + extra
        ).astype(jnp.bfloat16)

    row = lax.broadcasted_iota(jnp.int32, facts_ref.shape, 0)
    facts_ref[...] = jnp.where(row == 0, cells.astype(jnp.float32), jnp.where(row == 1, values_ref[...], 0.0))

    coefficients = coefficients_ref[...]
    weights = coefficients / jnp.sum(coefficients, axis=0, keepdims=True)
    tap = lax.broadcasted_iota(jnp.int32, (8, coefficients.shape[1]), 0)
    dense = jnp.zeros((8, coefficients.shape[1]), jnp.float32)
    for t in range(coefficients.shape[0]):
        dense = dense + jnp.where(tap == offsets_ref[t] + REACH, weights[t : t + 1, :], 0.0)
    for b in range(coefficients.shape[1] // LANES):
        taps_ref[b * LANES : (b + 1) * LANES, :] = dense[:, b * LANES : (b + 1) * LANES].T


def spread_weights(quarter, taps_ref, wide_ref):
    chunks = wide_ref.shape[1] // CHUNK // 4

    @pl.loop(quarter * chunks, (quarter + 1) * chunks)
    def _(i):
        rows = pl.ds(pl.multiple_of(i * CHUNK, CHUNK), CHUNK)
        block = taps_ref[rows, :]
        for j in range(TAPS):
            wide_ref[j, rows, :] = jnp.broadcast_to(block[:, j : j + 1], (CHUNK, LANES))


def start_panel(x_ref, first_column):
    groups, padded, _ = x_ref.shape
    cells = padded - 2 * PAD

    @pl.loop(0, padded // PAD)
    def _(i):
        row = i * PAD - PAD + lax.broadcasted_iota(jnp.int32, (PAD, LANES), 0)
        row = jnp.where(row < 0, row + cells, jnp.where(row >= cells, row - cells, row))
        column = first_column + lax.broadcasted_iota(jnp.int32, (PAD, LANES), 1)
        rows = pl.ds(pl.multiple_of(i * PAD, PAD), PAD)
        for g in range(groups - 1):
            x_ref[g, rows, :] = (row == column + g * LANES).astype(jnp.float32)
        x_ref[groups - 1, rows, :] = jnp.zeros((PAD, LANES), jnp.float32)


def spread(wide_ref, x_ref, y_ref, low_ref):
    groups, cells, _ = y_ref.shape

    @pl.loop(0, cells // CHUNK)
    def _(i):
        base = pl.multiple_of(i * CHUNK, CHUNK)
        rows = pl.ds(base, CHUNK)
        for g in range(groups):
            total = None
            for j in range(TAPS):
                part = wide_ref[j, rows, :] * x_ref[g, pl.ds(base + (PAD - REACH + j), CHUNK), :]
                total = part if total is None else total + part
            y_ref[g, rows, :] = total
            low_ref[rows, g * LANES : (g + 1) * LANES] = total.astype(jnp.bfloat16)


def mark(facts, hot_ref, forced_ref):
    obs, cells = hot_ref.shape
    columns = facts.T
    wanted = columns[:, 0:1].astype(jnp.int32)
    for b in range(cells // obs):
        ids = b * obs + lax.broadcasted_iota(jnp.int32, (obs, obs), 1)
        hot_ref[:, b * obs : (b + 1) * obs] = (ids == wanted).astype(jnp.bfloat16)
    lane = lax.broadcasted_iota(jnp.int32, (obs, LANES), 1)
    forced_ref[...] = jnp.where(lane == 0, -columns[:, 1:2], 0.0).astype(jnp.bfloat16)


def pick(hot_ref, forced_ref, low_ref, picked_ref):
    width = low_ref.shape[1]
    picked_ref[:, :width] = jnp.dot(
        hot_ref[...], low_ref[...], preferred_element_type=jnp.float32
    ).astype(jnp.bfloat16)
    picked_ref[:, width:] = forced_ref[...]


def correct(gains_ref, picked_ref, y_ref, store):
    groups = y_ref.shape[0]
    blocks, block, _ = gains_ref.shape

    @pl.loop(0, blocks)
    def _(i):
        base = pl.multiple_of(i * block, block)
        correction = jnp.dot(gains_ref[i], picked_ref[...], preferred_element_type=jnp.float32)
        for g in range(groups):
            value = y_ref[g, pl.ds(base, block), :] - correction[:, g * LANES : (g + 1) * LANES]
            if g == groups - 1:
                value = value - correction[:, groups * LANES :]
            store(g, base, block, value)


def scan_kernel(spans, ring, taps_ref, rows_ref, facts_ref, out_ref, offset_ref,
                gains, facts, wide_ref, x_ref, y_ref, low_ref, hot_ref, forced_ref, picked_ref,
                send_sem, recv_sem, local_sem):
    span, state = lax.axis_index("tm"), lax.axis_index("state")
    chip, core = state // 2, state % 2
    place = lambda step, which: lax.rem(chip + step, ring) * 2 + which
    right, left, far = (place(step, core) for step in (1, ring - 1, 2))
    twin = place(0, 1 - core)
    twin_of = lambda step: place(step, 1 - core)
    ahead, behind_span = lax.rem(span + 1, spans), lax.rem(span + spans - 1, spans)
    count = rows_ref.shape[0]
    half = count // 2
    whole, halves = (0, count), ((0, half), (half, half))
    quarters, rest = ((0, half // 2), (half // 2, half // 2)), halves[1]
    cells, groups = out_ref.shape[0], x_ref.shape[0]

    barrier = pltpu.get_barrier_semaphore()
    for there in ((span, right), (span, left), (span, twin), (ahead, state), (behind_span, state)):
        pl.semaphore_signal(barrier, inc=1, device_id=there, device_id_type=pl.DeviceIdType.MESH)
    pl.semaphore_wait(barrier, 5)

    def part(k, owner, rows):
        return gains.at[k, owner, pl.ds(*rows)]

    started = []

    def send(source, target, kind, k, there):
        copy = pltpu.make_async_remote_copy(
            src_ref=source, dst_ref=target, send_sem=send_sem.at[kind, k], recv_sem=recv_sem.at[kind, k],
            device_id=there, device_id_type=pl.DeviceIdType.MESH,
        )
        copy.start()
        started.append(copy)

    def arrive(target, kind, k):
        pltpu.make_async_remote_copy(
            src_ref=target, dst_ref=target, send_sem=send_sem.at[kind, k], recv_sem=recv_sem.at[kind, k],
            device_id=(span, twin), device_id_type=pl.DeviceIdType.MESH,
        ).wait_recv()

    def to_twin(k, owner, rows, kind):
        send(part(k, owner, rows), part(k, owner, rows), TWIN + kind, k, (span, twin))

    def go_ahead(k, h):
        rows = halves[h]
        source = rows_ref.at[pl.ds(*rows)] if k == 0 else part(k, state, rows)
        if h == 0:
            send(facts_ref if k == 0 else facts.at[k], facts.at[k + 1], FACTS, k + 1, (ahead, state))
        send(source, part(k + 1, state, rows), AHEAD + h, k + 1, (ahead, state))

    def take_ahead(k, h):
        if h == 0:
            arrive(facts.at[k], FACTS, k)
        arrive(part(k, state, halves[h]), AHEAD + h, k)
        if k < LEVELS - 1:
            go_ahead(k, h)

    def go_round(k):
        source = rows_ref if k == 0 else part(k, state, whole)
        send(source, part(k, state, whole), FROM_LEFT, k, (span, right))
        send(source, part(k, state, whole), FROM_RIGHT, k, (span, left))
        send(source, part(k, state, whole), TWIN + AHEAD, k, (span, twin))

    def take_sides(k):
        for owner, kind in ((left, FROM_LEFT), (right, FROM_RIGHT)):
            arrive(part(k, owner, whole), kind, k)
            to_twin(k, owner, whole, kind)

    def relay(k):
        first, second = quarters if k else halves
        send(part(k, left, first), part(k, left, first), FAR_LEFT, k, (span, right))
        send(part(k, right, second), part(k, right, second), FAR_RIGHT, k, (span, left))

    def far_ahead(k):
        send(part(k, far, rest), part(k + 1, far, rest), FAR_AHEAD, k + 1, (ahead, state))

    def take_far_ahead(k):
        arrive(part(k, far, rest), FAR_AHEAD, k)
        if k < LEVELS - 1:
            far_ahead(k)
        to_twin(k, far, rest, FAR_AHEAD)

    def take_far(k):
        for rows, kind in zip(quarters if k else halves, (FAR_LEFT, FAR_RIGHT)):
            arrive(part(k, far, rows), kind, k)
            to_twin(k, far, rows, kind)

    def take_twin(k):
        arrive(part(k, twin, whole), TWIN + AHEAD, k)
        arrive(part(k, twin_of(ring - 1), whole), TWIN + FROM_LEFT, k)
        arrive(part(k, twin_of(1), whole), TWIN + FROM_RIGHT, k)
        for rows, kind in zip(quarters if k else halves, (FAR_LEFT, FAR_RIGHT)):
            arrive(part(k, twin_of(2), rows), TWIN + kind, k)
        if k:
            arrive(part(k, twin_of(2), rest), TWIN + FAR_AHEAD, k)

    def keep(g, base, block, value):
        x_ref[g, pl.ds(base + PAD, block), :] = value

    def finish(g, base, block, value):
        if g < groups - 1:
            out_ref[pl.ds(base, block), g * LANES : (g + 1) * LANES] = value
        else:
            for piece in range(block // LANES):
                square = value[piece * LANES : (piece + 1) * LANES, :].T
                offset_ref[0:1, pl.ds(pl.multiple_of(base + piece * LANES, LANES), LANES)] = square[0:1, :]

    def look(k):
        def run():
            spread(wide_ref, x_ref, y_ref, low_ref)
            pick(hot_ref.at[k], forced_ref.at[k], low_ref, picked_ref)

        pl.when(span >= k)(run)

    def move(k):
        def run():
            correct(gains.at[k], picked_ref, y_ref, keep if k else finish)
            if k:
                for g in range(groups):
                    x_ref[g, 0:PAD, :] = x_ref[g, cells : cells + PAD, :]
                    x_ref[g, cells + PAD : cells + 2 * PAD, :] = x_ref[g, PAD : 2 * PAD, :]

        pl.when(span >= k)(run)

    def note(k):
        mark(facts_ref[...] if k == 0 else facts[k], hot_ref.at[k], forced_ref.at[k])

    def widen(quarter):
        spread_weights(quarter, taps_ref, wide_ref)

    go_ahead(0, 0)
    go_ahead(0, 1)
    go_round(0)
    own = pltpu.make_async_copy(rows_ref, gains.at[0, state], local_sem)
    own.start()
    start_panel(x_ref, state * out_ref.shape[1])
    note(0)
    widen(0)
    take_ahead(1, 0)
    widen(1)
    take_ahead(1, 1)
    go_round(1)
    take_sides(0)
    relay(0)
    note(1)
    take_ahead(2, 0)
    widen(2)
    take_ahead(2, 1)
    go_round(2)
    note(2)
    take_sides(1)
    take_ahead(3, 0)
    widen(3)
    take_ahead(3, 1)
    go_round(3)
    take_far(0)
    far_ahead(0)
    note(3)
    take_sides(2)
    look(3)
    take_far_ahead(1)
    take_sides(3)
    relay(3)
    relay(2)
    relay(1)
    take_far_ahead(2)
    take_far(3)
    take_far_ahead(3)
    take_twin(3)
    move(3)
    take_far(2)
    look(2)
    take_twin(2)
    move(2)
    take_far(1)
    look(1)
    take_twin(1)
    move(1)
    look(0)
    own.wait()
    take_twin(0)
    move(0)
    for copy in started:
        copy.wait_send()


def deliver_kernel(out_ref, offset_ref, out_final_ref, offset_final_ref, block_ref, line_ref, in_sem, done_sem):
    blocks, rows, _ = block_ref.shape
    pieces = [
        (out_ref.at[pl.ds(b * rows, rows)], block_ref.at[b], out_final_ref.at[pl.ds(b * rows, rows)])
        for b in range(blocks)
    ] + [(offset_ref, line_ref, offset_final_ref)]
    taken = [pltpu.make_async_copy(a, b, in_sem.at[n]) for n, (a, b, _) in enumerate(pieces)]
    given = [pltpu.make_async_copy(b, c, done_sem.at[n]) for n, (_, b, c) in enumerate(pieces)]
    for copy in taken:
        copy.start()
    for before, after in zip(taken, given):
        before.wait()
        after.start()
    for copy in given:
        copy.wait()


def shards(spans, states, offsets, coefficients, gain_matrix, direct_gain, observed_cells, observed_values):
    row_count, obs = gain_matrix.shape[2:]
    cells = coefficients.shape[1]
    rows, taps, facts = pl.pallas_call(
        prepare_kernel,
        out_shape=(
            jax.ShapeDtypeStruct((row_count, obs), jnp.bfloat16),
            jax.ShapeDtypeStruct((cells, 8), jnp.float32),
            jax.ShapeDtypeStruct((8, obs), jnp.float32),
        ),
        in_specs=[pl.BlockSpec(memory_space=pltpu.SMEM)] + [VMEM_SPEC] * 5,
        out_specs=(VMEM_SPEC,) * 3,
        name="prepare",
    )(offsets, coefficients, gain_matrix[0, 0], direct_gain[0], observed_cells[0], observed_values[0])
    groups = row_count // LANES + 1
    out, offset = pl.pallas_call(
        functools.partial(scan_kernel, spans, states // 2),
        out_shape=(
            jax.ShapeDtypeStruct((cells, row_count), jnp.float32),
            jax.ShapeDtypeStruct((1, cells), jnp.float32),
        ),
        in_specs=[VMEM_SPEC] * 3,
        out_specs=(VMEM_SPEC, VMEM_SPEC),
        scratch_shapes=[
            pltpu.VMEM((LEVELS, states, row_count, obs), jnp.bfloat16),
            pltpu.VMEM((LEVELS, 8, obs), jnp.float32),
            pltpu.VMEM((TAPS, cells, LANES), jnp.float32),
            pltpu.VMEM((groups, cells + 2 * PAD, LANES), jnp.float32),
            pltpu.VMEM((groups, cells, LANES), jnp.float32),
            pltpu.VMEM((cells, groups * LANES), jnp.bfloat16),
            pltpu.VMEM((LEVELS, obs, cells), jnp.bfloat16),
            pltpu.VMEM((LEVELS, obs, LANES), jnp.bfloat16),
            pltpu.VMEM((obs, (groups + 1) * LANES), jnp.bfloat16),
            pltpu.SemaphoreType.DMA((KINDS, LEVELS)),
            pltpu.SemaphoreType.DMA((KINDS, LEVELS)),
            pltpu.SemaphoreType.DMA,
        ],
        compiler_params=pltpu.CompilerParams(
            collective_id=0, has_side_effects=True, vmem_limit_bytes=56 * 1024 * 1024
        ),
        name="scan",
    )(taps, rows, facts)
    anywhere = pl.BlockSpec(memory_space=pl.ANY)
    blocks = 8
    out, offset = pl.pallas_call(
        deliver_kernel,
        out_shape=(
            jax.ShapeDtypeStruct(out.shape, out.dtype),
            jax.ShapeDtypeStruct(offset.shape, offset.dtype),
        ),
        in_specs=[anywhere] * 2,
        out_specs=(anywhere,) * 2,
        scratch_shapes=[
            pltpu.VMEM((blocks, cells // blocks, row_count), jnp.float32),
            pltpu.VMEM(offset.shape, jnp.float32),
            pltpu.SemaphoreType.DMA((blocks + 1,)),
            pltpu.SemaphoreType.DMA((blocks + 1,)),
        ],
        name="deliver",
    )(out, offset)
    return out[None], offset


def solution(mesh):
    in_specs = (
        P(),
        P(),
        P("tm", None, "state", None),
        P("tm", None, None),
        P("tm", None, None),
        P("tm", None, None),
    )
    out_specs = (P("tm", None, "state"), P("tm", None))
    run = functools.partial(shards, mesh.shape["tm"], mesh.shape["state"])
    return jax.shard_map(run, mesh=mesh, in_specs=in_specs, out_specs=out_specs, check_vma=False)
```
